32 devices in a mesh: ctx: 8 (over y, x, core), mp: 4 (over z).
Axes of the slice: x: 2, y: 2, z: 4, core: 2. Of those that a mesh axis runs over, the one named last changes fastest.
Arguments:
- tokens: bfloat16 [1, 4096, 4096], P(None, 'ctx', 'mp'), may hold values from -40 to 40
- w_branch: bfloat16 [4096, 2048], P(None, 'mp'), may hold values from -0.09375 to 0.09375
- w_input: bfloat16 [4096, 2048], P(None, 'mp'), may hold values from -0.09375 to 0.09375
- conv_kernel: float32 [4, 2048], P(None, 'mp'), may hold values from -3 to 3
- w_rate: bfloat16 [8, 256, 256], P('mp'), may hold values from -0.375 to 0.375
- w_admit: bfloat16 [8, 256, 256], P('mp'), may hold values from -0.375 to 0.375
- lam: float32 [2048], P('mp'), may hold values from 3 to 16
- w_out: bfloat16 [2048, 4096], P('mp'), may hold values from -0.375 to 0.375
- w_query: bfloat16 [4096, 2048], P(None, 'mp'), may hold values from -0.0625 to 0.0625
- w_key: bfloat16 [4096, 256], P(None, 'mp'), may hold values from -4.0625 to 4.0625
- w_value: bfloat16 [4096, 256], P(None, 'mp'), may hold values from -0.09375 to 0.09375
- w_attn_out: bfloat16 [2048, 4096], P('mp'), may hold values from -0.25 to 0.25
Outputs:
- layer_output: bfloat16 [1, 4096, 4096], P(None, 'ctx', 'mp')
The draws below stay inside these ranges and needn't reach their ends.
All inputs are finite; a program needn't handle non-finite values.
Results may differ from the reference program's by a relative error of at most 0.0065.
Values may be sent and summed in bfloat16 or wider, within the bound.
A program may use at most 128 MiB of HBM per device.

```python
import math
import jax
import jax.numpy as jnp
from jax import lax

D = 4096
LRU = 2048
BW = 256
NB = 8
HEADS = 8
HD = 256
CONV = 4
S_DEV = 512
WINDOW = 2048
B = 1
SEQ = 4096


def draw_tokens(key, part):
    base = jax.random.normal(jax.random.fold_in(key, 1), (B, SEQ, D), jnp.float32)
    base = jnp.clip(base, -4.0, 4.0)
    low = math.log(0.3)
    high = math.log(3.0)
    row_scale = jnp.exp(jax.random.uniform(jax.random.fold_in(key, 2), (B, SEQ, 1), jnp.float32, low, high))
    col_scale = jnp.exp(jax.random.uniform(jax.random.fold_in(key, 3), (1, 1, D), jnp.float32, low, high))
    return (base * row_scale * col_scale).astype(jnp.bfloat16)


def draw_lam(key, part):
    share = 0.5
    pick = jax.random.uniform(jax.random.fold_in(key, 21), (LRU,), jnp.float32)
    quick = 1.0 / jax.random.uniform(jax.random.fold_in(key, 22), (LRU,), jnp.float32, 30.0, 50.0)
    slow = jnp.exp(jax.random.uniform(jax.random.fold_in(key, 23), (LRU,), jnp.float32, math.log(0.2), math.log(2.0))) / SEQ
    rate = jnp.where(pick < share, quick, slow)
    return -jnp.log(jnp.expm1(rate / 4.0))


def query_matrix(key):
    drawn = jnp.clip(jax.random.normal(jax.random.fold_in(key, 31), (D, HEADS * HD), jnp.float32), -4.0, 4.0)
    return drawn / math.sqrt(D)


def draw_w_query(key, part):
    return query_matrix(key).astype(jnp.bfloat16)


def draw_w_key(key, part):
    own = jnp.clip(jax.random.normal(jax.random.fold_in(key, 32), (D, HD), jnp.float32), -4.0, 4.0) / math.sqrt(D)
    return own.astype(jnp.bfloat16)


def block_scale(own_key, dims, cuts, smallest, largest):
    factor_of = 1.0
    for dim, shards_of in cuts:
        heights = jax.random.uniform(jax.random.fold_in(jax.random.fold_in(own_key, 6), dim), (shards_of,), jnp.float32, smallest / len(cuts), largest / len(cuts))
        factor_of = factor_of * jnp.repeat(jnp.exp(heights), dims[dim] // shards_of).reshape((-1,) + (1,) * (len(dims) - 1 - dim))
    return factor_of


def scatter_about(rng, dims, scale, most, split=(), kind=jnp.bfloat16):
    values = scale * jax.random.normal(rng, dims, jnp.float32)
    if split:
        values = values * block_scale(rng, dims, split, -0.22, 0.18)
    return jnp.clip(values, -most, most).astype(kind)


def setup_inputs(seed: int = 0) -> dict:
    arg_keys = jax.random.split(jax.random.key(seed), 13)
    return {
        "tokens": draw_tokens(jax.random.fold_in(arg_keys[12], 71), 0),
        "w_branch": scatter_about(arg_keys[1], (D, LRU), D ** -0.5, 0.09375, ((1, 4),)),
        "w_input": scatter_about(arg_keys[2], (D, LRU), D ** -0.5, 0.09375, ((1, 4),)),
        "conv_kernel": scatter_about(arg_keys[3], (CONV, LRU), CONV ** -0.5, 3.0, ((1, 4),), jnp.float32),
        "w_rate": scatter_about(arg_keys[4], (NB, BW, BW), BW ** -0.5, 0.375, ((0, 4),)),
        "w_admit": scatter_about(arg_keys[5], (NB, BW, BW), BW ** -0.5, 0.375, ((0, 4),)),
        "lam": draw_lam(jax.random.fold_in(arg_keys[12], 71), 0),
        "w_out": scatter_about(arg_keys[7], (LRU, D), (LRU // 8) ** -0.5, 0.375, ((0, 4),)),
        "w_query": draw_w_query(jax.random.fold_in(arg_keys[12], 71), 0),
        "w_key": draw_w_key(jax.random.fold_in(arg_keys[12], 71), 0),
        "w_value": scatter_about(arg_keys[10], (D, HD), D ** -0.5, 0.09375, ((1, 4),)),
        "w_attn_out": scatter_about(arg_keys[11], (HEADS * HD, D), (HEADS * HD // 4) ** -0.5, 0.25, ((0, 4),)),
    }


def normalize(values):
    wide = values.astype(jnp.float32)
    return wide * lax.rsqrt(lax.optimization_barrier(jnp.mean(wide * wide, axis=-1, keepdims=True)) + 1e-06)

def rounded(values):
    return lax.optimization_barrier(values.astype(jnp.bfloat16)).astype(jnp.float32)

def rotate(values, positions):
    width = values.shape[-1]
    turned = width // 2
    half = turned // 2
    freqs = 10000.0 ** (-jnp.arange(half, dtype=jnp.float32) * 2.0 / turned)
    angles = positions.astype(jnp.float32)[:, None] * freqs[None, :]
    cosine = jnp.cos(angles)[:, None, :]
    sine = jnp.sin(angles)[:, None, :]
    first = values[..., :half]
    second = values[..., half:turned]
    return jnp.concatenate([first * cosine - second * sine, second * cosine + first * sine, values[..., turned:]], axis=-1)

def reference(tokens, w_branch, w_input, conv_kernel, w_rate, w_admit, lam, w_out, w_query, w_key, w_value, w_attn_out):
    count = B * SEQ
    normed = normalize(tokens).astype(jnp.bfloat16).reshape(count, D)
    branch = jax.nn.gelu(jnp.dot(normed, w_branch, preferred_element_type=jnp.float32))
    inner = jnp.dot(normed, w_input, preferred_element_type=jnp.float32).reshape(B, SEQ, LRU)
    padded = jnp.pad(inner, ((0, 0), (CONV - 1, 0), (0, 0)))
    convolved = jnp.zeros((B, SEQ, LRU), jnp.float32)
    for tap in range(CONV):
        convolved = convolved + conv_kernel[tap] * padded[:, CONV - 1 - tap:CONV - 1 - tap + SEQ, :]
    grouped = rounded(convolved).reshape(B, SEQ, NB, BW)
    rate_gate = jax.nn.sigmoid(jnp.einsum('bsnc,ncd->bsnd', grouped, w_rate.astype(jnp.float32))).reshape(B, SEQ, LRU)
    admit_gate = jax.nn.sigmoid(jnp.einsum('bsnc,ncd->bsnd', grouped, w_admit.astype(jnp.float32))).reshape(B, SEQ, LRU)
    log_decay = -8.0 * rate_gate * jax.nn.softplus(-lam)
    decay = jnp.exp(log_decay)
    scaled = admit_gate * convolved * jnp.sqrt(-jnp.expm1(2.0 * log_decay))

    def advance(carried, inputs):
        step_decay, step_input = inputs
        fresh = step_decay * carried + step_input
        return (fresh, fresh)
    _, states = lax.scan(advance, jnp.zeros((B, LRU), jnp.float32), (decay.transpose(1, 0, 2), scaled.transpose(1, 0, 2)))
    state = states.transpose(1, 0, 2)
    gated = (state.reshape(count, LRU) * branch).astype(jnp.bfloat16)
    resid = (tokens.reshape(count, D).astype(jnp.float32) + jnp.dot(gated, w_out, preferred_element_type=jnp.float32)).astype(jnp.bfloat16)
    normed_two = normalize(resid).astype(jnp.bfloat16)
    positions = jnp.arange(SEQ, dtype=jnp.int32)
    query = jnp.dot(normed_two, w_query, preferred_element_type=jnp.float32).reshape(B, SEQ, HEADS, HD)
    query = (rotate(query, positions) * HD ** (-0.5)).astype(jnp.bfloat16)
    key_raw = jnp.dot(normed_two, w_key, preferred_element_type=jnp.float32).astype(jnp.bfloat16)
    keys = rotate(key_raw.astype(jnp.float32).reshape(B, SEQ, 1, HD), positions).astype(jnp.bfloat16).reshape(B, SEQ, HD)
    values = jnp.dot(normed_two, w_value, preferred_element_type=jnp.float32).astype(jnp.bfloat16).reshape(B, SEQ, HD)
    key_pad = jnp.pad(keys, ((0, 0), (WINDOW, 0), (0, 0)))
    value_pad = jnp.pad(values, ((0, 0), (WINDOW, 0), (0, 0)))
    span = WINDOW + S_DEV

    def one_block(index):
        start = (index * S_DEV).astype(jnp.int32)
        query_block = lax.dynamic_slice_in_dim(query, start, S_DEV, 1).astype(jnp.float32)
        key_block = lax.dynamic_slice_in_dim(key_pad, start, span, 1).astype(jnp.float32)
        value_block = lax.dynamic_slice_in_dim(value_pad, start, span, 1).astype(jnp.float32)
        scores = jnp.einsum('bshc,bkc->bhsk', query_block, key_block)
        rows = jnp.arange(S_DEV, dtype=jnp.int32)[:, None]
        cols = jnp.arange(span, dtype=jnp.int32)[None, :]
        distance = rows + WINDOW - cols
        valid = (distance >= 0) & (distance < WINDOW) & (cols >= WINDOW - start)
        masked = jnp.where(valid, scores, -1e+30)
        top = lax.optimization_barrier(jnp.max(masked, axis=-1, keepdims=True))
        weights = jnp.where(valid, jnp.exp(masked - top), 0.0)
        probs = rounded(weights / lax.optimization_barrier(jnp.sum(weights, axis=-1, keepdims=True)))
        return jnp.einsum('bhsk,bkc->bshc', probs, value_block).astype(jnp.bfloat16)
    blocks = lax.map(one_block, jnp.arange(SEQ // S_DEV, dtype=jnp.int32))
    attended = blocks.transpose(1, 0, 2, 3, 4).reshape(count, HEADS * HD)
    result = resid.astype(jnp.float32) + jnp.dot(attended, w_attn_out, preferred_element_type=jnp.float32)
    return result.astype(jnp.bfloat16).reshape(B, SEQ, D)
```

```python
import functools

import jax
import jax.numpy as jnp
from jax import lax
from jax.experimental import pallas as pl
from jax.experimental.pallas import tpu as pltpu
from jax.sharding import PartitionSpec as P

HD = 256
WINDOW = 2048


EPSILON = 1e-06


def from_behind(x, axis, by):
    count = lax.axis_size(axis)
    pairs = [(i, i + by) for i in range(count) if 0 <= i + by < count]
    return lax.ppermute(x, axis, pairs)


def normalize(values):
    wide = values.astype(jnp.float32)
    return wide * lax.rsqrt(jnp.mean(wide * wide, axis=-1, keepdims=True) + EPSILON)


def rotate(values, positions):
    width = values.shape[-1]
    turned = width // 2
    half = turned // 2
    freqs = 10000.0 ** (-jnp.arange(half, dtype=jnp.float32) * 2.0 / turned)
    angles = positions.astype(jnp.float32)[:, None] * freqs[None, :]
    cosine = jnp.cos(angles)[:, None, :]
    sine = jnp.sin(angles)[:, None, :]
    first = values[..., :half]
    second = values[..., half:turned]
    return jnp.concatenate(
        [first * cosine - second * sine, second * cosine + first * sine, values[..., turned:]],
        axis=-1,
    )


def recurrence_kernel(
    count, decay_ref, scaled_ref, branch_ref, out_ref, local, cumulative, edge, got, send, recv
):
    me = lax.axis_index("ctx")
    barrier = pltpu.get_barrier_semaphore()
    for step in range(1, count):
        pl.semaphore_signal(barrier, inc=1, device_id={"ctx": lax.rem(me + step, count)})
    rows, width = decay_ref.shape
    tile = 8
    place = lax.broadcasted_iota(jnp.int32, (tile, width), 0)

    def advance(index, carried):
        state, product = carried
        at = pl.ds(pl.multiple_of(index * tile, tile), tile)
        a = decay_ref[at, :]
        b = scaled_ref[at, :]
        for shift in (1, 2, 4):
            inside = place >= shift
            a_back = jnp.where(inside, pltpu.roll(a, shift, 0), 1.0)
            b_back = jnp.where(inside, pltpu.roll(b, shift, 0), 0.0)
            b = a * b_back + b
            a = a * a_back
        b = b + a * state
        a = a * product
        local[at, :] = b
        cumulative[at, :] = a
        return b[tile - 1 :, :], a[tile - 1 :, :]

    start = (jnp.zeros((1, width), jnp.float32), jnp.ones((1, width), jnp.float32))
    state, product = lax.fori_loop(0, rows // tile, advance, start, unroll=4)
    edge[0:1, :] = state
    edge[1:2, :] = product
    pl.semaphore_wait(barrier, count - 1)
    copies = []
    for step in range(1, count):
        copy = pltpu.make_async_remote_copy(
            src_ref=edge,
            dst_ref=got.at[step],
            send_sem=send.at[step],
            recv_sem=recv.at[step],
            device_id={"ctx": lax.rem(me + step, count)},
        )
        copy.start()
        copies.append(copy)
    for copy in copies:
        copy.wait()
    carry = jnp.zeros((1, width), jnp.float32)
    for step in range(count - 1, 0, -1):
        fresh = got[step, 0:1, :] + got[step, 1:2, :] * carry
        carry = jnp.where(me >= step, fresh, 0.0)

    def finish(index, _):
        at = pl.ds(pl.multiple_of(index * 16, 16), 16)
        whole = local[at, :] + cumulative[at, :] * carry
        out_ref[at, :] = (whole * branch_ref[at, :]).astype(out_ref.dtype)
        return 0

    lax.fori_loop(0, rows // 16, finish, 0, unroll=4)


def recurrence(decay, scaled, branch):
    rows, width = decay.shape
    count = lax.axis_size("ctx")
    vmem = pl.BlockSpec(memory_space=pltpu.VMEM)
    return pl.pallas_call(
        functools.partial(recurrence_kernel, count),
        out_shape=jax.ShapeDtypeStruct((rows, width), jnp.bfloat16),
        in_specs=[vmem] * 3,
        out_specs=vmem,
        scratch_shapes=[
            pltpu.VMEM((rows, width), jnp.float32),
            pltpu.VMEM((rows, width), jnp.float32),
            pltpu.VMEM((2, width), jnp.float32),
            pltpu.VMEM((count, 2, width), jnp.float32),
            pltpu.SemaphoreType.DMA((count,)),
            pltpu.SemaphoreType.DMA((count,)),
        ],
        compiler_params=pltpu.CompilerParams(collective_id=0, has_side_effects=True),
    )(decay, scaled, branch)


def on_device(
    tokens,
    w_branch,
    w_input,
    conv_kernel,
    w_rate,
    w_admit,
    lam,
    w_out,
    w_query,
    w_key,
    w_value,
    w_attn_out,
):
    batch, rows_dev, cols_dev = tokens.shape
    count = batch * rows_dev
    width = w_branch.shape[0]
    full = lax.all_gather(tokens, "mp", axis=2, tiled=True)
    normed = normalize(full).astype(jnp.bfloat16).reshape(count, width)
    branch = jax.nn.gelu(jnp.dot(normed, w_branch, preferred_element_type=jnp.float32))
    inner = jnp.dot(normed, w_input, preferred_element_type=jnp.float32).reshape(
        batch, rows_dev, -1
    )
    taps = conv_kernel.shape[0]
    rim = from_behind(inner[:, rows_dev - taps + 1 :, :], "ctx", 1)
    extended = jnp.concatenate([rim, inner], axis=1)
    convolved = jnp.zeros_like(inner)
    for tap in range(taps):
        convolved = (
            convolved
            + conv_kernel[tap] * extended[:, taps - 1 - tap : taps - 1 - tap + rows_dev, :]
        )
    blocks = w_rate.shape[0]
    block_width = w_rate.shape[1]
    grouped = convolved.astype(jnp.bfloat16).reshape(batch, rows_dev, blocks, block_width)
    rate_gate = jax.nn.sigmoid(
        jnp.einsum("bsnc,ncd->bsnd", grouped, w_rate, preferred_element_type=jnp.float32)
    ).reshape(batch, rows_dev, -1)
    admit_gate = jax.nn.sigmoid(
        jnp.einsum("bsnc,ncd->bsnd", grouped, w_admit, preferred_element_type=jnp.float32)
    ).reshape(batch, rows_dev, -1)
    log_decay = -8.0 * rate_gate * jax.nn.softplus(-lam)
    decay = jnp.exp(log_decay)
    scaled = admit_gate * convolved * jnp.sqrt(-jnp.expm1(2.0 * log_decay))
    channels = decay.shape[-1]
    gated = recurrence(
        decay.reshape(count, channels), scaled.reshape(count, channels), branch
    )
    partial_out = jnp.dot(gated, w_out, preferred_element_type=jnp.float32)
    share = lax.psum_scatter(
        partial_out.astype(jnp.bfloat16).reshape(batch, rows_dev, width),
        "mp",
        scatter_dimension=2,
        tiled=True,
    )
    resid_share = (tokens.astype(jnp.float32) + share.astype(jnp.float32)).astype(jnp.bfloat16)
    resid = lax.all_gather(resid_share, "mp", axis=2, tiled=True)
    normed_two = normalize(resid).astype(jnp.bfloat16).reshape(count, width)
    base = lax.axis_index("ctx") * rows_dev
    positions = base + jnp.arange(rows_dev, dtype=jnp.int32)
    key_local = jnp.dot(normed_two, w_key, preferred_element_type=jnp.float32).astype(jnp.bfloat16)
    value_local = jnp.dot(normed_two, w_value, preferred_element_type=jnp.float32).astype(
        jnp.bfloat16
    )
    both = lax.all_gather(jnp.stack([key_local, value_local]), "mp", axis=2, tiled=True)
    key_raw, value_whole = both[0], both[1]
    query = jnp.dot(normed_two, w_query, preferred_element_type=jnp.float32).reshape(
        batch, rows_dev, -1, HD
    )
    query = (rotate(query, positions) * HD ** (-0.5)).astype(jnp.bfloat16)
    keys = (
        rotate(key_raw.astype(jnp.float32).reshape(batch, rows_dev, 1, HD), positions)
        .astype(jnp.bfloat16)
        .reshape(batch, rows_dev, HD)
    )
    paired = jnp.stack([keys, value_whole.reshape(batch, rows_dev, HD)])
    earlier = [from_behind(paired, "ctx", distance) for distance in (4, 3, 2, 1)]
    window_kv = jnp.concatenate(earlier + [paired], axis=2)
    span = window_kv.shape[2]
    scores = jnp.einsum("bshc,bkc->bhsk", query, window_kv[0], preferred_element_type=jnp.float32)
    rows = jnp.arange(rows_dev, dtype=jnp.int32)[:, None]
    cols = jnp.arange(span, dtype=jnp.int32)[None, :]
    distance_back = rows + WINDOW - cols
    valid = (distance_back >= 0) & (distance_back < WINDOW) & (cols >= WINDOW - base)
    masked = jnp.where(valid, scores, -1e30)
    top = jnp.max(masked, axis=-1, keepdims=True)
    weights = jnp.where(valid, jnp.exp(masked - top), 0.0)
    probs = (weights / jnp.sum(weights, axis=-1, keepdims=True)).astype(jnp.bfloat16)
    attended = (
        jnp.einsum("bhsk,bkc->bshc", probs, window_kv[1], preferred_element_type=jnp.float32)
        .astype(jnp.bfloat16)
        .reshape(count, -1)
    )
    partial_attn = jnp.dot(attended, w_attn_out, preferred_element_type=jnp.float32)
    share_attn = lax.psum_scatter(
        partial_attn.reshape(batch, rows_dev, width).astype(jnp.bfloat16),
        "mp",
        scatter_dimension=2,
        tiled=True,
    ).astype(jnp.float32)
    return (resid_share.astype(jnp.float32) + share_attn).astype(jnp.bfloat16)


def solution(mesh):
    in_specs = (
        P(None, "ctx", "mp"),
        P(None, "mp"),
        P(None, "mp"),
        P(None, "mp"),
        P("mp", None, None),
        P("mp", None, None),
        P("mp"),
        P("mp", None),
        P(None, "mp"),
        P(None, "mp"),
        P(None, "mp"),
        P("mp", None),
    )
    out_specs = P(None, "ctx", "mp")
    return jax.shard_map(
        on_device, mesh=mesh, in_specs=in_specs, out_specs=out_specs, check_vma=False
    )
```

```python
import functools

import jax
import jax.numpy as jnp
from jax import lax
from jax.experimental import pallas as pl
from jax.experimental.pallas import tpu as pltpu
from jax.sharding import PartitionSpec as P

HD = 256
WINDOW = 2048


EPSILON = 1e-06


def from_behind(x, axis, by):
    count = lax.axis_size(axis)
    pairs = [(i, i + by) for i in range(count) if 0 <= i + by < count]
    return lax.ppermute(x, axis, pairs)


def normalize(values):
    wide = values.astype(jnp.float32)
    return wide * lax.rsqrt(jnp.mean(wide * wide, axis=-1, keepdims=True) + EPSILON)


def rotate(values, positions):
    width = values.shape[-1]
    turned = width // 2
    half = turned // 2
    freqs = 10000.0 ** (-jnp.arange(half, dtype=jnp.float32) * 2.0 / turned)
    angles = positions.astype(jnp.float32)[:, None] * freqs[None, :]
    cosine = jnp.cos(angles)[:, None, :]
    sine = jnp.sin(angles)[:, None, :]
    first = values[..., :half]
    second = values[..., half:turned]
    return jnp.concatenate(
        [first * cosine - second * sine, second * cosine + first * sine, values[..., turned:]],
        axis=-1,
    )


def recurrence_kernel(
    count, decay_ref, scaled_ref, branch_ref, out_ref, local, cumulative, edge, got, send, recv
):
    me = lax.axis_index("ctx")
    barrier = pltpu.get_barrier_semaphore()
    for step in range(1, count):
        pl.semaphore_signal(barrier, inc=1, device_id={"ctx": lax.rem(me + step, count)})
    rows, width = decay_ref.shape
    tile = 8
    place = lax.broadcasted_iota(jnp.int32, (tile, width), 0)

    def advance(index, carried):
        state, product = carried
        at = pl.ds(pl.multiple_of(index * tile, tile), tile)
        a = decay_ref[at, :]
        b = scaled_ref[at, :]
        for shift in (1, 2, 4):
            inside = place >= shift
            a_back = jnp.where(inside, pltpu.roll(a, shift, 0), 1.0)
            b_back = jnp.where(inside, pltpu.roll(b, shift, 0), 0.0)
            b = a * b_back + b
            a = a * a_back
        b = b + a * state
        a = a * product
        local[at, :] = b
        cumulative[at, :] = a
        return b[tile - 1 :, :], a[tile - 1 :, :]

    start = (jnp.zeros((1, width), jnp.float32), jnp.ones((1, width), jnp.float32))
    state, product = lax.fori_loop(0, rows // tile, advance, start, unroll=4)
    edge[0:1, :] = state
    edge[1:2, :] = product
    pl.semaphore_wait(barrier, count - 1)
    copies = []
    for step in range(1, count):
        copy = pltpu.make_async_remote_copy(
            src_ref=edge,
            dst_ref=got.at[step],
            send_sem=send.at[step],
            recv_sem=recv.at[step],
            device_id={"ctx": lax.rem(me + step, count)},
        )
        copy.start()
        copies.append(copy)
    for copy in copies:
        copy.wait()
    carry = jnp.zeros((1, width), jnp.float32)
    for step in range(count - 1, 0, -1):
        fresh = got[step, 0:1, :] + got[step, 1:2, :] * carry
        carry = jnp.where(me >= step, fresh, 0.0)

    def finish(index, _):
        at = pl.ds(pl.multiple_of(index * 16, 16), 16)
        whole = local[at, :] + cumulative[at, :] * carry
        out_ref[at, :] = (whole * branch_ref[at, :]).astype(out_ref.dtype)
        return 0

    lax.fori_loop(0, rows // 16, finish, 0, unroll=4)


def recurrence(decay, scaled, branch):
    rows, width = decay.shape
    count = lax.axis_size("ctx")
    vmem = pl.BlockSpec(memory_space=pltpu.VMEM)
    return pl.pallas_call(
        functools.partial(recurrence_kernel, count),
        out_shape=jax.ShapeDtypeStruct((rows, width), jnp.bfloat16),
        in_specs=[vmem] * 3,
        out_specs=vmem,
        scratch_shapes=[
            pltpu.VMEM((rows, width), jnp.float32),
            pltpu.VMEM((rows, width), jnp.float32),
            pltpu.VMEM((2, width), jnp.float32),
            pltpu.VMEM((count, 2, width), jnp.float32),
            pltpu.SemaphoreType.DMA((count,)),
            pltpu.SemaphoreType.DMA((count,)),
        ],
        compiler_params=pltpu.CompilerParams(collective_id=0, has_side_effects=True),
    )(decay, scaled, branch)


CHUNKS = 4


def greet(me, count):
    barrier = pltpu.get_barrier_semaphore()
    for step in range(1, count):
        pl.semaphore_signal(barrier, inc=1, device_id={"mp": lax.rem(me + step, count)})
    pl.semaphore_wait(barrier, count - 1)


def each(chunks, body):
    def turn(chunk, _):
        body(chunk)
        return 0

    lax.fori_loop(0, chunks, turn, 0)


def span_of(chunk, rows):
    return pl.ds(pl.multiple_of(chunk * rows, rows), rows)


class Line:
    def __init__(self, me, count):
        self.me, self.count = me, count

    def steps(self, way):
        return self.me + 1 if way == 0 else self.me - 1

    def has_next(self, way):
        return self.me < self.count - 1 if way == 0 else self.me > 0

    def has_last(self, way):
        return self.me > 0 if way == 0 else self.me < self.count - 1

    def copy(self, way, src, dst, send, recv):
        return pltpu.make_async_remote_copy(
            src_ref=src,
            dst_ref=dst,
            send_sem=send,
            recv_sem=recv,
            device_id={"mp": self.steps(way)},
        )


def gather_part(line, own, out_ref, send, recv, cols, rows, chunks):
    me, count = line.me, line.count

    def region(owner, chunk):
        return out_ref.at[
            span_of(chunk, rows), pl.ds(pl.multiple_of(owner * cols, cols), cols)
        ]

    def source(way, step):
        return me - step if way == 0 else me + step

    def moved(way, step, chunk):
        owner = source(way, step)
        place = region(owner, chunk)
        return line.copy(
            way,
            own.at[span_of(chunk, rows), :] if step == 0 else place,
            place,
            send.at[way, step, chunk],
            recv.at[way, step, chunk],
        )

    def there(way, step):
        return source(way, step) >= 0 if way == 0 else source(way, step) < count

    def begin(chunk):
        for way in (0, 1):

            @pl.when(line.has_next(way))
            def _():
                moved(way, 0, chunk).start()

    def relay():
        for step in range(1, count):

            def turn(chunk, step=step):
                for way in (0, 1):

                    @pl.when(there(way, step))
                    def _():
                        place = region(source(way, step), chunk)
                        line.copy(
                            1 - way,
                            place,
                            place,
                            send.at[way, step - 1, chunk],
                            recv.at[way, step - 1, chunk],
                        ).wait_recv()

                    @pl.when(jnp.logical_and(there(way, step), line.has_next(way)))
                    def _():
                        moved(way, step, chunk).start()

            each(chunks, turn)

        for step in range(count):

            def turn(chunk, step=step):
                for way in (0, 1):

                    @pl.when(jnp.logical_and(there(way, step), line.has_next(way)))
                    def _():
                        moved(way, step, chunk).wait_send()

            each(chunks, turn)

    return region, begin, relay


def reduce_part(line, part_ref, base_ref, held, send, recv, cols, rows, chunks):
    me, count = line.me, line.count

    def goal(way, step):
        return count - 1 - step if way == 0 else step

    def beyond(way, step):
        return goal(way, step) > me if way == 0 else goal(way, step) < me

    def moved(way, step, chunk):
        place = held.at[way, step, span_of(chunk, rows), :]
        return line.copy(
            way,
            held.at[way, step, span_of(chunk, rows), :],
            place,
            send.at[way, step, chunk],
            recv.at[way, step, chunk],
        )

    def arrived(way, step, chunk):
        place = held.at[way, step, span_of(chunk, rows), :]
        line.copy(
            1 - way, place, place, send.at[way, step, chunk], recv.at[way, step, chunk]
        ).wait_recv()

    def term(owner, chunk):
        return part_ref[
            span_of(chunk, rows), pl.ds(pl.multiple_of(owner * cols, cols), cols)
        ]

    def outward():
        for step in range(count - 1):

            def turn(chunk, step=step):
                for way in (0, 1):
                    at = span_of(chunk, rows)

                    @pl.when(jnp.logical_and(beyond(way, step), line.has_last(way)))
                    def _():
                        arrived(way, step, chunk)
                        total = held[way, step, at, :].astype(jnp.float32) + term(
                            goal(way, step), chunk
                        ).astype(jnp.float32)
                        held[way, step, at, :] = total.astype(held.dtype)

                    @pl.when(
                        jnp.logical_and(
                            beyond(way, step), jnp.logical_not(line.has_last(way))
                        )
                    )
                    def _():
                        held[way, step, at, :] = term(goal(way, step), chunk)

                    @pl.when(beyond(way, step))
                    def _():
                        moved(way, step, chunk).start()

            each(chunks, turn)

    def finish(chunk, total):
        at = span_of(chunk, rows)
        total[...] = term(me, chunk).astype(jnp.float32)
        for way in (0, 1):
            for step in range(count):

                @pl.when(jnp.logical_and(goal(way, step) == me, line.has_last(way)))
                def _():
                    arrived(way, step, chunk)
                    total[...] += held[way, step, at, :].astype(jnp.float32)

        return (base_ref[at, :].astype(jnp.float32) + total[...]).astype(jnp.bfloat16)

    def settle():
        for step in range(count - 1):

            def turn(chunk, step=step):
                for way in (0, 1):

                    @pl.when(beyond(way, step))
                    def _():
                        moved(way, step, chunk).wait_send()

            each(chunks, turn)

    return outward, finish, settle


def gather_kernel(count, chunks, own_ref, out_ref, send, recv, local):
    me = lax.axis_index("mp")
    rows, cols = own_ref.shape[0] // chunks, own_ref.shape[1]
    greet(me, count)
    line = Line(me, count)
    region, begin, relay = gather_part(line, own_ref, out_ref, send, recv, cols, rows, chunks)

    def turn(chunk):
        begin(chunk)

    each(chunks, turn)
    mine = out_ref.at[:, pl.ds(pl.multiple_of(me * cols, cols), cols)]
    kept = pltpu.make_async_copy(own_ref, mine, local.at[0])
    kept.start()
    relay()
    kept.wait()


def reduce_gather_kernel(
    count, chunks, part_ref, base_ref, own_ref, out_ref, held, total, sends, recvs, send, recv, local
):
    me = lax.axis_index("mp")
    rows, cols = base_ref.shape[0] // chunks, base_ref.shape[1]
    greet(me, count)
    line = Line(me, count)
    outward, finish, settle = reduce_part(
        line, part_ref, base_ref, held, sends, recvs, cols, rows, chunks
    )
    region, begin, relay = gather_part(line, own_ref, out_ref, send, recv, cols, rows, chunks)
    outward()

    def turn(chunk):
        own_ref[span_of(chunk, rows), :] = finish(chunk, total)
        begin(chunk)

    each(chunks, turn)
    mine = out_ref.at[:, pl.ds(pl.multiple_of(me * cols, cols), cols)]
    kept = pltpu.make_async_copy(own_ref, mine, local.at[0])
    kept.start()
    relay()
    settle()
    kept.wait()


def reduce_kernel(count, chunks, part_ref, base_ref, own_ref, held, total, sends, recvs):
    me = lax.axis_index("mp")
    rows, cols = base_ref.shape[0] // chunks, base_ref.shape[1]
    greet(me, count)
    line = Line(me, count)
    outward, finish, settle = reduce_part(
        line, part_ref, base_ref, held, sends, recvs, cols, rows, chunks
    )
    outward()

    def turn(chunk):
        own_ref[span_of(chunk, rows), :] = finish(chunk, total)

    each(chunks, turn)
    settle()


def gather(own, mark, chunks=CHUNKS):
    count = lax.axis_size("mp")
    rows, cols = own.shape
    return pl.pallas_call(
        functools.partial(gather_kernel, count, chunks),
        out_shape=jax.ShapeDtypeStruct((rows, cols * count), own.dtype),
        in_specs=[pl.BlockSpec(memory_space=pltpu.VMEM)],
        out_specs=pl.BlockSpec(memory_space=pl.ANY),
        scratch_shapes=[
            pltpu.SemaphoreType.DMA((2, count, chunks)),
            pltpu.SemaphoreType.DMA((2, count, chunks)),
            pltpu.SemaphoreType.DMA((1,)),
        ],
        compiler_params=pltpu.CompilerParams(collective_id=mark, has_side_effects=True),
    )(own)


def reduce_scatter(part, base, mark, spread, chunks=CHUNKS):
    count = lax.axis_size("mp")
    rows, cols = base.shape
    vmem = pl.BlockSpec(memory_space=pltpu.VMEM)
    own = jax.ShapeDtypeStruct((rows, cols), base.dtype)
    semaphores = pltpu.SemaphoreType.DMA((2, count, chunks))
    scratch = [
        pltpu.VMEM((2, count, rows, cols), base.dtype),
        pltpu.VMEM((rows // chunks, cols), jnp.float32),
        semaphores,
        semaphores,
    ]
    if spread:
        return pl.pallas_call(
            functools.partial(reduce_gather_kernel, count, chunks),
            out_shape=(own, jax.ShapeDtypeStruct((rows, cols * count), base.dtype)),
            in_specs=[vmem, vmem],
            out_specs=(vmem, pl.BlockSpec(memory_space=pl.ANY)),
            scratch_shapes=scratch + [semaphores, semaphores, pltpu.SemaphoreType.DMA((1,))],
            compiler_params=pltpu.CompilerParams(collective_id=mark, has_side_effects=True),
        )(part, base)
    return pl.pallas_call(
        functools.partial(reduce_kernel, count, chunks),
        out_shape=own,
        in_specs=[vmem, vmem],
        out_specs=vmem,
        scratch_shapes=scratch,
        compiler_params=pltpu.CompilerParams(collective_id=mark, has_side_effects=True),
    )(part, base)


def on_device(
    tokens,
    w_branch,
    w_input,
    conv_kernel,
    w_rate,
    w_admit,
    lam,
    w_out,
    w_query,
    w_key,
    w_value,
    w_attn_out,
):
    batch, rows_dev, cols_dev = tokens.shape
    count = batch * rows_dev
    width = w_branch.shape[0]
    tokens_flat = tokens.reshape(count, cols_dev)
    full = gather(tokens_flat, 1)
    normed = normalize(full).astype(jnp.bfloat16).reshape(count, width)
    branch = jax.nn.gelu(jnp.dot(normed, w_branch, preferred_element_type=jnp.float32))
    inner = jnp.dot(normed, w_input, preferred_element_type=jnp.float32).reshape(
        batch, rows_dev, -1
    )
    taps = conv_kernel.shape[0]
    rim = from_behind(inner[:, rows_dev - taps + 1 :, :], "ctx", 1)
    extended = jnp.concatenate([rim, inner], axis=1)
    convolved = jnp.zeros_like(inner)
    for tap in range(taps):
        convolved = (
            convolved
            + conv_kernel[tap] * extended[:, taps - 1 - tap : taps - 1 - tap + rows_dev, :]
        )
    blocks = w_rate.shape[0]
    block_width = w_rate.shape[1]
    low = convolved.astype(jnp.bfloat16).reshape(count, -1)

    def gate(weights):
        products = [
            jnp.dot(
                low[:, block * block_width : (block + 1) * block_width],
                weights[block],
                preferred_element_type=jnp.float32,
            )
            for block in range(blocks)
        ]
        return jax.nn.sigmoid(jnp.concatenate(products, axis=-1)).reshape(batch, rows_dev, -1)

    rate_gate = gate(w_rate)
    admit_gate = gate(w_admit)
    log_decay = -8.0 * rate_gate * jax.nn.softplus(-lam)
    decay = jnp.exp(log_decay)
    scaled = admit_gate * convolved * jnp.sqrt(-jnp.expm1(2.0 * log_decay))
    channels = decay.shape[-1]
    gated = recurrence(
        decay.reshape(count, channels), scaled.reshape(count, channels), branch
    )
    partial_out = jnp.dot(gated, w_out, preferred_element_type=jnp.float32)
    resid_share, resid = reduce_scatter(
        partial_out.astype(jnp.bfloat16), tokens_flat, 2, spread=True
    )
    normed_two = normalize(resid).astype(jnp.bfloat16).reshape(count, width)
    base = lax.axis_index("ctx") * rows_dev
    positions = base + jnp.arange(rows_dev, dtype=jnp.int32)
    key_local = jnp.dot(normed_two, w_key, preferred_element_type=jnp.float32).astype(jnp.bfloat16)
    value_local = jnp.dot(normed_two, w_value, preferred_element_type=jnp.float32).astype(
        jnp.bfloat16
    )
    both = lax.all_gather(jnp.stack([key_local, value_local]), "mp", axis=2, tiled=True)
    key_raw, value_whole = both[0], both[1]
    query = jnp.dot(normed_two, w_query, preferred_element_type=jnp.float32).reshape(
        batch, rows_dev, -1, HD
    )
    query = (rotate(query, positions) * HD ** (-0.5)).astype(jnp.bfloat16)
    keys = (
        rotate(key_raw.astype(jnp.float32).reshape(batch, rows_dev, 1, HD), positions)
        .astype(jnp.bfloat16)
        .reshape(batch, rows_dev, HD)
    )
    paired = jnp.stack([keys, value_whole.reshape(batch, rows_dev, HD)])
    earlier = [from_behind(paired, "ctx", distance) for distance in (4, 3, 2, 1)]
    window_kv = jnp.concatenate(earlier + [paired], axis=2)
    span = window_kv.shape[2]
    scores = jnp.einsum("bshc,bkc->bhsk", query, window_kv[0], preferred_element_type=jnp.float32)
    rows = jnp.arange(rows_dev, dtype=jnp.int32)[:, None]
    cols = jnp.arange(span, dtype=jnp.int32)[None, :]
    distance_back = rows + WINDOW - cols
    valid = (distance_back >= 0) & (distance_back < WINDOW) & (cols >= WINDOW - base)
    masked = jnp.where(valid, scores, -1e30)
    top = jnp.max(masked, axis=-1, keepdims=True)
    weights = jnp.where(valid, jnp.exp(masked - top), 0.0)
    probs = (weights / jnp.sum(weights, axis=-1, keepdims=True)).astype(jnp.bfloat16)
    attended = (
        jnp.einsum("bhsk,bkc->bshc", probs, window_kv[1], preferred_element_type=jnp.float32)
        .astype(jnp.bfloat16)
        .reshape(count, -1)
    )
    partial_attn = jnp.dot(attended, w_attn_out, preferred_element_type=jnp.float32)
    result = reduce_scatter(partial_attn.astype(jnp.bfloat16), resid_share, 3, spread=False)
    return result.reshape(batch, rows_dev, cols_dev)


def solution(mesh):
    in_specs = (
        P(None, "ctx", "mp"),
        P(None, "mp"),
        P(None, "mp"),
        P(None, "mp"),
        P("mp", None, None),
        P("mp", None, None),
        P("mp"),
        P("mp", None),
        P(None, "mp"),
        P(None, "mp"),
        P(None, "mp"),
        P("mp", None),
    )
    out_specs = P(None, "ctx", "mp")
    return jax.shard_map(
        on_device, mesh=mesh, in_specs=in_specs, out_specs=out_specs, check_vma=False
    )
```
